128 devices in a mesh: front: 8 (over z, core), grid: 16 (over y, x).
Axes of the slice: x: 4, y: 4, z: 4, core: 2. Of those that a mesh axis runs over, the one named last changes fastest.
Arguments:
- pivot_block: float32 [8, 512, 512], P('front'), as said below
- border: float32 [8, 8192, 512], P('front', 'grid'), may hold values from -0.9 to 0.9
- trailing: float32 [8, 8192, 8192], P('front', 'grid'), as said below
- dest_owner: int32 [8, 2560, 1], P('front', 'grid'), may hold values from 0 to 127; in each aligned block of 160 rows (0 to 159, 160 to 319, ..., all dimensions but the last counted through in order) at most 2 rows name the same one
- dest_slot: int32 [8, 2560], P('front', 'grid'), may hold values from 0 to 63
- row_map: int32 [8, 2560, 128], P('front', 'grid'), may hold values from 0 to 127, each once within a row
Outputs:
- pivot_factor: float32 [8, 512, 512], P('front')
- border_factor: float32 [8, 8192, 512], P('front', 'grid')
- ancestor_blocks: float32 [8192, 128, 128], P(('front', 'grid'))
The draws below stay inside these ranges and needn't reach their ends.
Inputs may be any that keep to these rules, and one draw needn't show every extreme that they name: `pivot_block`: symmetric positive definite. `trailing`: Symmetric. `dest_owner`: in each aligned block of 160 entries no owner is named more than 2 times, a bound that some block reaches.
All inputs are finite; a program needn't handle non-finite values.
Results may differ from the reference program's by a relative error of at most 0.0001.
Values sent between devices are 32-bit elements; how exact they have to be, the bound alone decides.
A program may use at most 192 MiB of HBM per device.

```python
import math
import jax
import jax.numpy as jnp
import numpy as np
from jax import lax

BLK = 128
NB = 256
P_SIZE = 512
M = 8192
SLOTS = 64
FRONTS = 8
TILES_DEV = 160
TILES = 2560
CAP = 2
N_GRID = 16
DEVICES = 128


def draw_pivot_block(key, part):
    first_key, second_key = jax.random.split(jax.random.fold_in(key, 11))
    noise = jnp.clip(jax.random.normal(first_key, (FRONTS, P_SIZE, P_SIZE), jnp.float32), -3.0, 3.0)
    diagonal = jnp.exp(jax.random.uniform(second_key, (FRONTS, P_SIZE), jnp.float32, 0.41, 1.79))
    offdiag = (noise + jnp.swapaxes(noise, 1, 2)) * (0.3 / jnp.sqrt(2.0 * P_SIZE))
    identity = jnp.eye(P_SIZE, dtype=jnp.float32)
    return offdiag * (1.0 - identity) + identity * diagonal[:, None, :]


def draw_trailing(key, part):
    first_key = jax.random.fold_in(key, 23)
    noise = jax.random.normal(first_key, (FRONTS, M, M), jnp.float32)
    return (noise + jnp.swapaxes(noise, 1, 2)) * 0.7071


def with_ends(entries, own_key, low, top_value):
    shape = entries.shape
    index_at = [jax.random.randint(jax.random.fold_in(own_key, axis), (), 0, shape[axis]) for axis in range(len(shape))]
    entries = entries.at[tuple(index_at)].set(low)
    longest = shape.index(max(shape))
    index_at[longest] = (index_at[longest] + 1) % shape[longest]
    return entries.at[tuple(index_at)].set(top_value)


def level_of(key, extent, cuts, low, high):
    loudness, own = 1.0, jax.random.fold_in(key, 6)
    for position, shards_of in cuts:
        steps = jnp.exp(jax.random.uniform(jax.random.fold_in(own, position), (shards_of,), jnp.float32, low / len(cuts), high / len(cuts)))
        loudness = loudness * jnp.repeat(steps, extent[position] // shards_of).reshape([-1 if axis == position else 1 for axis in range(len(extent))])
    return loudness


def shared_out(own_key, own, number, rows, count, top, reach, skew):
    ranking = jax.random.permutation(own_key, count)
    crowded, usual = load_shares(count, rows * top, reach, skew, True), load_shares(count, rows * top, reach, skew, False)
    places = jnp.arange(count)

    def named(lengths, offset_by):
        used = int((lengths > 0).sum())
        fixed = max(1, used // 4)
        shifted = fixed + (places - fixed + offset_by * (used - fixed)) % max(1, count - fixed)
        return jnp.zeros((count,), jnp.int32).at[ranking[jnp.where(places < fixed, places, shifted)]].set(jnp.asarray(lengths, jnp.int32))

    lengths = jnp.where(number % 4 == 0, named(crowded, number // 4), named(usual, number - number // 4 - 1))
    mixed = jax.random.permutation(jax.random.fold_in(own, 3), count)
    giver, receiver = mixed[0:count // 2 * 2:2], mixed[1:count // 2 * 2:2]
    slack = jnp.minimum(lengths[giver] - 1, reach - lengths[receiver]) // 2
    slack = jnp.where((giver == ranking[0]) | (receiver == ranking[0]) | (lengths[receiver] == 0), 0, jnp.maximum(slack, 0))
    shifted = jax.random.randint(jax.random.fold_in(own, 4), (count // 2,), 0, 1 << 20) % (slack + 1)
    lengths = lengths.at[giver].add(-shifted).at[receiver].add(shifted)
    labels = jnp.searchsorted(jnp.cumsum(lengths), jnp.arange(rows * top), side="right").astype(jnp.int32)
    table = labels.reshape(top, rows).T
    table = table[jax.random.permutation(jax.random.fold_in(own, 1), rows)]
    offset_by = jax.random.randint(jax.random.fold_in(own, 2), (rows, 1), 0, top)
    return jnp.take_along_axis(table, (jnp.arange(top)[None, :] + offset_by) % top, axis=1)


def load_shares(count, total, reach, slope, full):
    loads = [(1 << 20) // math.isqrt(rank ** slope) + 1 for rank in range(1, count + 1)]
    largest = reach if full else min(reach, max(-(-total // count), total * loads[0] // sum(loads)))
    least = 1 if total - largest >= count - 1 else 0
    holding, spare = [largest] + [least] * (count - 1), total - largest - least * (count - 1)
    while spare > 0:
        candidates = [i for i in range(1, count) if holding[i] < largest] or [i for i in range(1, count) if holding[i] < reach]
        whole, left = sum([loads[i] for i in candidates]), spare
        for i in candidates:
            addition = min(reach - holding[i], max(1, left * loads[i] // whole), spare)
            holding[i] = holding[i] + addition
            spare = spare - addition
    return np.array(holding)


def bell_draw(key, shape, spread, bound, shards=(), kind=jnp.bfloat16):
    loudness = level_of(key, shape, shards, -0.22, 0.18) if shards else 1.0
    values = jax.random.normal(key, shape, jnp.float32) * spread * loudness
    return jnp.minimum(jnp.maximum(values, -bound), bound).astype(kind)


def setup_inputs(seed: int = 0) -> dict:
    key_of = jax.random.split(jax.random.key(seed), 7)
    pivot_block = draw_pivot_block(jax.random.fold_in(key_of[6], 71), 0)
    border = bell_draw(key_of[1], (FRONTS, M, P_SIZE), 0.15, 0.9, ((0, 8), (1, 16)), jnp.float32)
    trailing = draw_trailing(jax.random.fold_in(key_of[6], 71), 0)
    dest_owner_keys = jax.random.split(jax.random.fold_in(key_of[3], 1), FRONTS * TILES // TILES_DEV)
    dest_owner_turns = jax.random.permutation(jax.random.fold_in(key_of[3], 3), FRONTS * TILES // TILES_DEV)
    dest_owner = jax.vmap(lambda own, number: shared_out(jax.random.fold_in(key_of[3], 2), own, number, TILES_DEV, DEVICES, 1, CAP, 2))(dest_owner_keys, dest_owner_turns).reshape((FRONTS, TILES, 1))
    dest_slot = with_ends(jax.random.randint(key_of[4], (FRONTS, TILES), 0, SLOTS), jax.random.fold_in(key_of[4], 1), 0, SLOTS - 1).astype(jnp.int32)
    row_map = jax.vmap(lambda own: jax.random.permutation(own, BLK))(jax.random.split(key_of[5], FRONTS * TILES)).reshape((FRONTS, TILES, BLK)).astype(jnp.int32)
    return {"pivot_block": pivot_block, "border": border, "trailing": trailing, "dest_owner": dest_owner, "dest_slot": dest_slot, "row_map": row_map}


precise = lax.Precision.HIGHEST

def factor_panels(corner, border_rows_in):
    first_factor = jnp.linalg.cholesky(corner[:NB, :NB])
    remainder = jnp.concatenate([corner[NB:, :NB], border_rows_in[:, :NB]], axis=0)
    solved = jax.scipy.linalg.solve_triangular(first_factor, remainder.T, lower=True).T
    pivot_rows = solved[:NB]
    border_rows = solved[NB:]
    updated_pivot = corner[NB:, NB:] - jnp.dot(pivot_rows, pivot_rows.T, precision=precise)
    updated_border = border_rows_in[:, NB:] - jnp.dot(border_rows, pivot_rows.T, precision=precise)
    second_factor = jnp.linalg.cholesky(updated_pivot)
    second_border = jax.scipy.linalg.solve_triangular(second_factor, updated_border.T, lower=True).T
    upper_half = jnp.concatenate([first_factor, jnp.zeros((NB, NB), jnp.float32)], axis=1)
    lower_half = jnp.concatenate([pivot_rows, second_factor], axis=1)
    return (jnp.concatenate([upper_half, lower_half], axis=0), jnp.concatenate([border_rows, second_border], axis=1))

def tile_table():
    per_dev = M // (N_GRID * BLK)
    blocks_all = M // BLK
    row_list = []
    col_list = []
    alive_list = []
    for member in range(N_GRID):
        count_live = 0
        for local_index in range(per_dev):
            true_row = local_index * N_GRID + member
            for column in range(blocks_all):
                if column % per_dev * N_GRID + column // per_dev <= true_row:
                    row_list.append(member * per_dev + local_index)
                    col_list.append(column)
                    alive_list.append(1.0)
                    count_live += 1
        for padding in range(TILES_DEV - count_live):
            row_list.append(0)
            col_list.append(0)
            alive_list.append(0.0)
    return (np.array(row_list, np.int32), np.array(col_list, np.int32), np.array(alive_list, np.float32))

def reference(pivot_block, border, trailing, dest_owner, dest_slot, row_map):
    row_table, col_table, alive_table = tile_table()
    alive_weight = jnp.asarray(alive_table).astype(jnp.float32)
    targets = jnp.zeros((DEVICES * SLOTS, BLK, BLK), jnp.float32)
    pivot_all = []
    border_all = []
    for front in range(FRONTS):
        pivot_factor, border_factor = factor_panels(pivot_block[front], border[front])
        pivot_all.append(pivot_factor)
        border_all.append(border_factor)
        contribution = trailing[front] - jnp.dot(border_factor, border_factor.T, precision=precise)
        blocked = contribution.reshape(M // BLK, BLK, M // BLK, BLK)
        picked = blocked[jnp.asarray(row_table), :, jnp.asarray(col_table), :] * alive_weight[:, None, None]
        moved = jnp.take_along_axis(picked, row_map[front][:, :, None], axis=1)
        target_index = (dest_owner[front, :, 0] * SLOTS + dest_slot[front]).astype(jnp.int32)
        targets = targets.at[target_index].add(moved)
    return (jnp.stack(pivot_all), jnp.stack(border_all), targets)
```

```python
import functools

import jax
import jax.numpy as jnp
import numpy as np
from jax import lax
from jax.experimental import pallas as pl
from jax.experimental.pallas import tpu as pltpu
from jax.sharding import PartitionSpec as P

BLK = 128
SLOTS = 64
N_GRID = 16
GROUP = 4
P_SIZE = 512
HI = lax.Precision.HIGHEST
VMEM = pl.BlockSpec(memory_space=pltpu.VMEM)


def tdot(a, b):
    return lax.dot_general(a, b, (((0,), (0,)), ((), ())), precision=HI, preferred_element_type=jnp.float32)


def factor_diagonal(block):
    aug = jnp.concatenate([block, jnp.eye(BLK, dtype=jnp.float32)], axis=1)
    sub = lax.broadcasted_iota(jnp.int32, (8, BLK), 0)
    sub2 = lax.broadcasted_iota(jnp.int32, (8, 2 * BLK), 0)
    done = []
    for panel in range(BLK // 8):
        rows = aug[:8]
        cols = [jnp.broadcast_to(rows[:, 8 * panel + m : 8 * panel + m + 1], (8, BLK)) for m in range(8)]
        for i in range(8):
            inv = lax.rsqrt(jnp.broadcast_to(cols[i][i : i + 1], (8, BLK)))
            mult = jnp.where(sub > i, cols[i] * inv, 0.0)
            inv2 = jnp.concatenate([inv, inv], axis=1)
            mult2 = jnp.concatenate([mult, mult], axis=1)
            top = jnp.broadcast_to(rows[i : i + 1], (8, 2 * BLK)) * inv2
            rows = jnp.where(sub2 == i, top, rows - mult2 * top)
            for m in range(i + 1, 8):
                cols[m] = cols[m] - mult * (jnp.broadcast_to(cols[m][i : i + 1], (8, BLK)) * inv)
        done.append(rows)
        if panel < BLK // 8 - 1:
            left = rows[:, :BLK]
            update = tdot(left, rows)
            aug = aug[8:] - update[8 * (panel + 1) :]
    full = jnp.concatenate(done, axis=0)
    r = lax.broadcasted_iota(jnp.int32, (BLK, BLK), 0)
    c = lax.broadcasted_iota(jnp.int32, (BLK, BLK), 1)
    return jnp.where(r <= c, full[:, :BLK], 0.0), full[:, BLK:]


def factor_kernel(a_ref, b_ref, pivot_ref, border_ref, whi_ref, wlo_ref, aug_ref):
    r = lax.broadcasted_iota(jnp.int32, (P_SIZE, P_SIZE), 0)
    c = lax.broadcasted_iota(jnp.int32, (P_SIZE, P_SIZE), 1)
    aug_ref[:, :P_SIZE] = a_ref[...]
    aug_ref[:, P_SIZE:] = jnp.where(r == c, 1.0, 0.0)
    lane = lax.broadcasted_iota(jnp.int32, (BLK, 2 * P_SIZE), 1)

    def step(b, _):
        start = pl.multiple_of(b * BLK, BLK)
        stripe = aug_ref[pl.ds(start, BLK), :]
        diag = aug_ref[pl.ds(start, BLK), pl.ds(start, BLK)]
        upper, inverse = factor_diagonal(diag)
        solved = jnp.dot(inverse, stripe, precision=HI, preferred_element_type=jnp.float32)
        solved = jnp.where(lane >= start, solved, 0.0)
        aug_ref[pl.ds(start, BLK), :] = solved
        aug_ref[pl.ds(start, BLK), pl.ds(start, BLK)] = upper

        def rest(k, _):
            at = pl.multiple_of(k * BLK, BLK)
            left = aug_ref[pl.ds(start, BLK), pl.ds(at, BLK)]
            aug_ref[pl.ds(at, BLK), :] = aug_ref[pl.ds(at, BLK), :] - tdot(left, aug_ref[pl.ds(start, BLK), :])
            return 0

        lax.fori_loop(b + 1, P_SIZE // BLK, rest, 0)
        return 0

    lax.fori_loop(0, P_SIZE // BLK, step, 0)
    pivot_ref[...] = jnp.where(r >= c, aug_ref[:, :P_SIZE].T, 0.0)
    inverse = jnp.where(r >= c, aug_ref[:, P_SIZE:], 0.0)
    solved = lax.dot_general(b_ref[...], inverse, (((1,), (1,)), ((), ())), precision=HI, preferred_element_type=jnp.float32)
    border_ref[...] = solved
    weights = jnp.dot(solved, inverse, precision=HI, preferred_element_type=jnp.float32)
    high = weights.astype(jnp.bfloat16)
    whi_ref[...] = high
    wlo_ref[...] = (weights - high.astype(jnp.float32)).astype(jnp.bfloat16)


def factor(a, b):
    sq = jax.ShapeDtypeStruct((P_SIZE, P_SIZE), jnp.float32)
    half = jax.ShapeDtypeStruct((P_SIZE, P_SIZE), jnp.bfloat16)
    return pl.pallas_call(
        factor_kernel,
        out_shape=(sq, sq, half, half),
        in_specs=[VMEM, VMEM],
        out_specs=(VMEM, VMEM, VMEM, VMEM),
        scratch_shapes=[pltpu.VMEM((P_SIZE, 2 * P_SIZE), jnp.float32)],
        compiler_params=pltpu.CompilerParams(vmem_limit_bytes=32 << 20),
        name="factor",
    )(a, b)


def tile_table():
    per_dev = 8192 // (N_GRID * BLK)
    table = np.full((N_GRID, 160), -1, np.int32)
    for member in range(N_GRID):
        place = 0
        for local in range(per_dev):
            for column in range(8192 // BLK):
                if column % per_dev * N_GRID + column // per_dev <= local * N_GRID + member:
                    table[member, place] = local * (8192 // BLK) + column
                    place += 1
    return table


def tiles_kernel(tile_ref, entry_ref, whi_ref, wlo_ref, map_ref, *refs):
    trailing = refs[:GROUP]
    border = refs[GROUP : 2 * GROUP]
    out_ref = refs[2 * GROUP]
    step = pl.program_id(0)
    for t in range(GROUP):
        tile = tile_ref[step * GROUP + t]
        entry = entry_ref[step * GROUP + t]

        @pl.when(tile >= 0)
        def _(t=t, tile=tile, entry=entry):
            at = pl.multiple_of(tile // 64 * BLK, BLK)
            cols = border[t][...]
            high = cols.astype(jnp.bfloat16)
            low = (cols - high.astype(jnp.float32)).astype(jnp.bfloat16)
            left_high = whi_ref[pl.ds(at, BLK), :]
            left = jnp.concatenate([left_high, left_high, wlo_ref[pl.ds(at, BLK), :]], axis=1)
            right = jnp.concatenate([high, low, high], axis=1)
            product = lax.dot_general(left, right, (((1,), (1,)), ((), ())), preferred_element_type=jnp.float32)
            value = trailing[t][...] - product
            upper = value.astype(jnp.bfloat16)
            lower = (value - upper.astype(jnp.float32)).astype(jnp.bfloat16)
            source = jnp.broadcast_to(map_ref[pl.ds(entry, 1), :], (BLK, BLK))
            chosen = source == lax.broadcasted_iota(jnp.int32, (BLK, BLK), 0)
            chosen = jnp.where(chosen, 1.0, 0.0).astype(jnp.bfloat16)
            moved = lax.dot_general(chosen, jnp.concatenate([upper, lower], axis=1), (((0,), (0,)), ((), ())), preferred_element_type=jnp.float32)
            out_ref[t] = moved[:, :BLK] + moved[:, BLK:]


def tiles(tile, entry, whi, wlo, row_map, trailing, border_all):
    def trailing_map(t):
        def index(i, tile_ref, entry_ref):
            at = jnp.maximum(tile_ref[i * GROUP + t], 0)
            return at // 64, at % 64
        return index

    def border_map(t):
        def index(i, tile_ref, entry_ref):
            return jnp.maximum(tile_ref[i * GROUP + t], 0) % 64, 0
        return index

    def whole(i, tile_ref, entry_ref):
        return 0, 0

    count = tile.shape[0]
    return pl.pallas_call(
        tiles_kernel,
        out_shape=jax.ShapeDtypeStruct((count, BLK, BLK), jnp.float32),
        grid_spec=pltpu.PrefetchScalarGridSpec(
            num_scalar_prefetch=2,
            grid=(count // GROUP,),
            in_specs=[
                pl.BlockSpec((P_SIZE, P_SIZE), whole),
                pl.BlockSpec((P_SIZE, P_SIZE), whole),
                pl.BlockSpec((160, BLK), whole),
            ]
            + [pl.BlockSpec((BLK, BLK), trailing_map(t)) for t in range(GROUP)]
            + [pl.BlockSpec((BLK, P_SIZE), border_map(t)) for t in range(GROUP)],
            out_specs=pl.BlockSpec((GROUP, BLK, BLK), lambda i, tile_ref, entry_ref: (i, 0, 0)),
        ),
        compiler_params=pltpu.CompilerParams(vmem_limit_bytes=40 << 20),
        cost_estimate=pl.CostEstimate(flops=count * 2 * BLK * BLK * 1792, transcendentals=0, bytes_accessed=count * 384 * 1024),
        name="tiles",
    )(tile, entry, whi, wlo, row_map, *([trailing] * GROUP), *([border_all] * GROUP))


def sum_kernel(first, slot_ref, *refs):
    arrived_ref, out_ref = refs[-2:]
    step = pl.program_id(0)

    @pl.when(step == 0)
    def _():
        out_ref[...] = jnp.zeros_like(out_ref) if first else refs[0][...]

    for t in range(8):
        slot = slot_ref[step * 8 + t]

        @pl.when(slot >= 0)
        def _(t=t, slot=slot):
            out_ref[slot] = out_ref[slot] + arrived_ref[t]


def slot_sums(slot, arrived, before=None):
    count = arrived.shape[0]
    whole = pl.BlockSpec((SLOTS, BLK, BLK), lambda i, slot_ref: (0, 0, 0))
    first = before is None
    return pl.pallas_call(
        functools.partial(sum_kernel, first),
        out_shape=jax.ShapeDtypeStruct((SLOTS, BLK, BLK), jnp.float32),
        grid_spec=pltpu.PrefetchScalarGridSpec(
            num_scalar_prefetch=1,
            grid=(count // 8,),
            in_specs=([] if first else [whole]) + [pl.BlockSpec((8, BLK, BLK), lambda i, slot_ref: (i, 0, 0))],
            out_specs=whole,
        ),
        compiler_params=pltpu.CompilerParams(vmem_limit_bytes=40 << 20),
        cost_estimate=pl.CostEstimate(flops=count * BLK * BLK, transcendentals=0, bytes_accessed=count * 64 * 1024),
        name="slot_sums",
    )(slot, *([] if first else [before]), arrived)


def body(pivot_block, border, trailing, dest_owner, dest_slot, row_map):
    border_all = lax.all_gather(border[0], "grid", axis=0, tiled=True)
    pivot_factor, border_factor, whi, wlo = factor(pivot_block[0], border[0])
    member = lax.axis_index("grid")
    devices = lax.axis_size("front") * lax.axis_size("grid")
    listed = dest_owner.shape[1]
    table = jnp.asarray(tile_table())[member]
    owner = dest_owner[0, :, 0]
    hits = (owner[:, None] == jnp.arange(devices, dtype=jnp.int32)[None, :]) & (table >= 0)[:, None]
    counted = hits.astype(jnp.int32)
    before = jnp.arange(listed)[:, None] > jnp.arange(listed)[None, :]
    later = jnp.dot(before.astype(jnp.bfloat16), counted.astype(jnp.bfloat16), preferred_element_type=jnp.float32) > 0.5
    entries = jnp.arange(listed, dtype=jnp.int32)[:, None]
    ranked = []
    for rank in range(2):
        chosen = hits & (later == (rank == 1))
        ranked.append((
            jnp.sum(jnp.where(chosen, table[:, None] + 1, 0), axis=0) - 1,
            jnp.sum(jnp.where(chosen, entries, 0), axis=0),
            jnp.sum(jnp.where(chosen, dest_slot[0][:, None] + 1, 0), axis=0) - 1,
        ))
    slots = lax.all_to_all(jnp.stack([ranked[0][2], ranked[1][2]], axis=1), ("front", "grid"), split_axis=0, concat_axis=0, tiled=True)
    arrived = []
    for rank in range(2):
        tile, entry, _ = ranked[rank]
        moved = tiles(tile, entry, whi, wlo, row_map[0], trailing[0], border_all)
        arrived.append(lax.all_to_all(moved, ("front", "grid"), split_axis=0, concat_axis=0, tiled=True))
    sums = slot_sums(slots[:, 0], arrived[0])
    sums = slot_sums(slots[:, 1], arrived[1], sums)
    return pivot_factor[None], border_factor[None], sums


def solution(mesh):
    return jax.shard_map(
        body,
        mesh=mesh,
        in_specs=(
            P("front", None, None),
            P("front", "grid", None),
            P("front", "grid", None),
            P("front", "grid", None),
            P("front", "grid"),
            P("front", "grid", None),
        ),
        out_specs=(
            P("front", None, None),
            P("front", "grid", None),
            P(("front", "grid"), None, None),
        ),
        check_vma=False,
    )
```

```python
import functools

import jax
import jax.numpy as jnp
import numpy as np
from jax import lax
from jax.experimental import pallas as pl
from jax.experimental.pallas import tpu as pltpu
from jax.sharding import PartitionSpec as P

BLK = 128
SLOTS = 64
N_GRID = 16
SIDE = 4
TILES_DEV = 160
SUM_GROUP = 8
P_SIZE = 512
HI = lax.Precision.HIGHEST
VMEM = pl.BlockSpec(memory_space=pltpu.VMEM)
ANY = pl.BlockSpec(memory_space=pl.ANY)
MESH = pl.DeviceIdType.MESH
HALF = P_SIZE // 2


def tdot(a, b):
    return lax.dot_general(a, b, (((0,), (0,)), ((), ())), precision=HI, preferred_element_type=jnp.float32)


def factor_diagonal(block):
    aug = jnp.concatenate([block, jnp.eye(BLK, dtype=jnp.float32)], axis=1)
    sub = lax.broadcasted_iota(jnp.int32, (8, BLK), 0)
    sub2 = lax.broadcasted_iota(jnp.int32, (8, 2 * BLK), 0)
    done = []
    for panel in range(BLK // 8):
        rows = aug[:8]
        cols = [jnp.broadcast_to(rows[:, 8 * panel + m : 8 * panel + m + 1], (8, BLK)) for m in range(8)]
        for i in range(8):
            inv = lax.rsqrt(jnp.broadcast_to(cols[i][i : i + 1], (8, BLK)))
            mult = jnp.where(sub > i, cols[i] * inv, 0.0)
            inv2 = jnp.concatenate([inv, inv], axis=1)
            mult2 = jnp.concatenate([mult, mult], axis=1)
            top = jnp.broadcast_to(rows[i : i + 1], (8, 2 * BLK)) * inv2
            rows = jnp.where(sub2 == i, top, rows - mult2 * top)
            for m in range(i + 1, 8):
                cols[m] = cols[m] - mult * (jnp.broadcast_to(cols[m][i : i + 1], (8, BLK)) * inv)
        done.append(rows)
        if panel < BLK // 8 - 1:
            left = rows[:, :BLK]
            update = tdot(left, rows)
            aug = aug[8:] - update[8 * (panel + 1) :]
    full = jnp.concatenate(done, axis=0)
    r = lax.broadcasted_iota(jnp.int32, (BLK, BLK), 0)
    c = lax.broadcasted_iota(jnp.int32, (BLK, BLK), 1)
    return jnp.where(r <= c, full[:, :BLK], 0.0), full[:, BLK:]


def front_kernel(
    a_ref, b_ref, t_ref, map_ref,
    pivot_ref, border_ref, out_ref,
    aug_ref, all_ref, left_ref, right_ref, tile_ref, moved_ref,
    send_sem, recv_sem, local_sem, tile_sem, moved_sem,
):
    front, member = lax.axis_index("front"), lax.axis_index("grid")
    place = (member % SIDE, member // SIDE)

    def at(offset):
        return (place[1] + offset[1]) % SIDE * SIDE + (place[0] + offset[0]) % SIDE

    def along(half, first, second):
        return (first, second) if half == 0 else (second, first)

    def piece(half, source, quarter):
        start, size = (half * HALF, HALF) if quarter is None else (half * HALF + quarter * BLK, BLK)
        return all_ref.at[source, pl.ds(start, size)]

    def copy(half, kind, source, quarter, target):
        part = piece(half, source, quarter)
        return pltpu.make_async_remote_copy(
            src_ref=part, dst_ref=part, send_sem=send_sem.at[half, kind], recv_sem=recv_sem.at[half, kind],
            device_id=(front, target), device_id_type=MESH,
        )

    def send(half, kind, first, second, quarter, step):
        copy(half, kind, at(along(half, first, second)), quarter, at(step)).start()

    def arrived(half, kind, first, second, quarter):
        copy(half, kind, at(along(half, first, second)), quarter, member).wait_recv()

    def open_own():
        for half in range(2):
            send(half, 0, 0, 0, None, along(half, 1, 0))
            send(half, 1, 0, 0, None, along(half, 3, 0))
        for half in range(2):
            second_axis(half, 0)

    def second_axis(half, d):
        send(half, 4 + d, d, 0, None, along(half, 0, 1))
        send(half, 8 + d, d, 0, None, along(half, 0, 3))

    def pass_on(half, d):
        arrived(half, 4 + d, d, 3, None)
        send(half, 12 + d, d, 3, 0, along(half, 0, 1))
        arrived(half, 8 + d, d, 1, None)
        send(half, 16 + d, d, 1, 1, along(half, 0, 3))

    def stage_first():
        for half in range(2):
            arrived(half, 0, 3, 0, None)
            send(half, 2, 3, 0, 0, along(half, 1, 0))
            arrived(half, 1, 1, 0, None)
            send(half, 3, 1, 0, 1, along(half, 3, 0))
        for half in range(2):
            second_axis(half, 3)
            second_axis(half, 1)

    def stage_second():
        for half in range(2):
            arrived(half, 2, 2, 0, 0)
            arrived(half, 3, 2, 0, 1)
            second_axis(half, 2)
        for half in range(2):
            pass_on(half, 0)

    def stage_third():
        for half in range(2):
            pass_on(half, 3)
            pass_on(half, 1)

    def stage_fourth():
        for half in range(2):
            pass_on(half, 2)

    barrier = pltpu.get_barrier_semaphore()
    neighbours = [at((1, 0)), at((3, 0)), at((0, 1)), at((0, 3))]
    for target in neighbours:
        pl.semaphore_signal(barrier, inc=1, device_id=(front, target), device_id_type=MESH)
    own = pltpu.make_async_copy(b_ref, all_ref.at[member], local_sem)
    own.start()
    own.wait()
    pl.semaphore_wait(barrier, 4)
    open_own()

    r = lax.broadcasted_iota(jnp.int32, (P_SIZE, P_SIZE), 0)
    c = lax.broadcasted_iota(jnp.int32, (P_SIZE, P_SIZE), 1)
    aug_ref[:, :P_SIZE] = a_ref[...]
    aug_ref[:, P_SIZE:] = jnp.where(r == c, 1.0, 0.0)
    lane = lax.broadcasted_iota(jnp.int32, (BLK, 2 * P_SIZE), 1)

    def step(b, _):
        start = pl.multiple_of(b * BLK, BLK)
        stripe = aug_ref[pl.ds(start, BLK), :]
        diag = aug_ref[pl.ds(start, BLK), pl.ds(start, BLK)]
        upper, inverse = factor_diagonal(diag)
        solved = jnp.dot(inverse, stripe, precision=HI, preferred_element_type=jnp.float32)
        solved = jnp.where(lane >= start, solved, 0.0)
        aug_ref[pl.ds(start, BLK), :] = solved
        aug_ref[pl.ds(start, BLK), pl.ds(start, BLK)] = upper

        def rest(k, _):
            row = pl.multiple_of(k * BLK, BLK)
            left = aug_ref[pl.ds(start, BLK), pl.ds(row, BLK)]
            aug_ref[pl.ds(row, BLK), :] = aug_ref[pl.ds(row, BLK), :] - tdot(left, aug_ref[pl.ds(start, BLK), :])
            return 0

        lax.fori_loop(b + 1, P_SIZE // BLK, rest, 0)
        for when, stage in enumerate((stage_first, stage_second, stage_third, stage_fourth)):
            pl.when(b == when)(stage)
        return 0

    lax.fori_loop(0, P_SIZE // BLK, step, 0)

    def source_of(i):
        u, v = i % SIDE, i // SIDE
        rx = u + u // 2 - 2 * (u // 3)
        ry = v + v // 2 - 2 * (v // 3)
        return at((rx, ry)), rx, ry, u, v

    def tile_copy(i, slot):
        column = pl.multiple_of(source_of(i)[0] * P_SIZE, P_SIZE)
        return pltpu.make_async_copy(t_ref.at[:, pl.ds(column, P_SIZE)], tile_ref.at[slot], tile_sem.at[slot])

    tile_copy(0, 0).start()
    inverse = jnp.where(r >= c, aug_ref[:, P_SIZE:], 0.0)
    pivot_ref[...] = jnp.where(r >= c, aug_ref[:, :P_SIZE].T, 0.0)
    own_rows = all_ref[member]
    solved = lax.dot_general(own_rows, inverse, (((1,), (1,)), ((), ())), precision=HI, preferred_element_type=jnp.float32)
    border_ref[...] = solved
    weights = jnp.dot(solved, inverse, precision=HI, preferred_element_type=jnp.float32)
    high = weights.astype(jnp.bfloat16)
    left_ref[:, :P_SIZE] = high
    left_ref[:, P_SIZE : 2 * P_SIZE] = high
    left_ref[:, 2 * P_SIZE :] = (weights - high.astype(jnp.float32)).astype(jnp.bfloat16)

    def moved_wait(slot):
        pltpu.make_async_copy(moved_ref.at[slot], out_ref.at[pl.ds(0, 10)], moved_sem.at[slot]).wait()

    def source_step(i, _):
        slot = i % 2
        source, rx, ry, u, v = source_of(i)

        @pl.when(i + 1 < N_GRID)
        def _():
            tile_copy(i + 1, 1 - slot).start()

        @pl.when(u == 3)
        def _():
            arrived(1, 12 + ry, ry, 2, 0)
            arrived(1, 16 + ry, ry, 2, 1)

        @pl.when(v == 3)
        def _():
            arrived(0, 12 + rx, rx, 2, 0)
            arrived(0, 16 + rx, rx, 2, 1)

        rows = all_ref[source]
        upper = rows.astype(jnp.bfloat16)
        right_ref[:, :P_SIZE] = upper
        right_ref[:, P_SIZE : 2 * P_SIZE] = (rows - upper.astype(jnp.float32)).astype(jnp.bfloat16)
        right_ref[:, 2 * P_SIZE :] = upper
        tile_copy(i, slot).wait()

        @pl.when(i >= 2)
        def _():
            moved_wait(slot)

        past = (source - member + N_GRID - 1) // N_GRID
        full = source - past * (source - member - 1)
        listed = 100 + 4 * member
        count = 0
        for pair in range(2):
            low = pair * HALF
            product = lax.dot_general(
                left_ref[low:, :], right_ref[low : low + HALF, :], (((1,), (1,)), ((), ())),
                preferred_element_type=jnp.float32,
            )
            tile_ref[slot, low:, low : low + HALF] = tile_ref[slot, low:, low : low + HALF] - product
            for k in range(2 * pair, 4):
                for m in range(2 * pair, min(2 * pair + 1, k) + 1):
                    entry = 8 * k * (k - 1) + k * (member + 1) + source * k + full + m
                    if m == k:
                        entry = entry + past * (listed + k * (N_GRID - 1 - member) + source - member - 1 - entry)
                    value = tile_ref[slot, k * BLK : (k + 1) * BLK, m * BLK : (m + 1) * BLK]
                    first = value.astype(jnp.bfloat16)
                    last = (value - first.astype(jnp.float32)).astype(jnp.bfloat16)
                    wanted = jnp.broadcast_to(map_ref[pl.ds(entry, 1), :], (BLK, BLK))
                    chosen = wanted == lax.broadcasted_iota(jnp.int32, (BLK, BLK), 0)
                    chosen = jnp.where(chosen, 1.0, 0.0).astype(jnp.bfloat16)
                    moved = lax.dot_general(
                        chosen, jnp.concatenate([first, last], axis=1), (((0,), (0,)), ((), ())),
                        preferred_element_type=jnp.float32,
                    )
                    moved_ref[slot, count] = moved[:, :BLK] + moved[:, BLK:]
                    pltpu.make_async_copy(moved_ref.at[slot, count], out_ref.at[entry], moved_sem.at[slot]).start()
                    count += 1
        return 0

    lax.fori_loop(0, N_GRID, source_step, 0)
    moved_wait(0)
    moved_wait(1)
    for half in range(2):
        for kind in range(20):
            quarter = None if kind < 2 or 4 <= kind < 12 else 0
            copy(half, kind, member, quarter, member).wait_send()


def front_tiles(pivot_block, border, trailing, row_map):
    square = jax.ShapeDtypeStruct((P_SIZE, P_SIZE), jnp.float32)
    return pl.pallas_call(
        front_kernel,
        out_shape=(square, square, jax.ShapeDtypeStruct((TILES_DEV, BLK, BLK), jnp.float32)),
        in_specs=[VMEM, ANY, ANY, VMEM],
        out_specs=(VMEM, VMEM, ANY),
        scratch_shapes=[
            pltpu.VMEM((P_SIZE, 2 * P_SIZE), jnp.float32),
            pltpu.VMEM((N_GRID, P_SIZE, P_SIZE), jnp.float32),
            pltpu.VMEM((P_SIZE, 3 * P_SIZE), jnp.bfloat16),
            pltpu.VMEM((P_SIZE, 3 * P_SIZE), jnp.bfloat16),
            pltpu.VMEM((2, P_SIZE, P_SIZE), jnp.float32),
            pltpu.VMEM((2, 10, BLK, BLK), jnp.float32),
            pltpu.SemaphoreType.DMA((2, 20)),
            pltpu.SemaphoreType.DMA((2, 20)),
            pltpu.SemaphoreType.DMA,
            pltpu.SemaphoreType.DMA((2,)),
            pltpu.SemaphoreType.DMA((2,)),
        ],
        compiler_params=pltpu.CompilerParams(collective_id=0, has_side_effects=True, vmem_limit_bytes=52 << 20),
        name="front_tiles",
    )(pivot_block, border, trailing, row_map)


def spread_kernel(owner_ref, rank_ref, tiles_ref, note_ref, out_ref, held_ref, in_sem, out_sem, note_sem):
    chunk = TILES_DEV // 8
    notes = pltpu.make_async_copy(note_ref, out_ref.at[:, pl.ds(2 * BLK, 8)], note_sem)
    notes.start()

    def load(i):
        part = pl.ds(i * chunk, chunk)
        return pltpu.make_async_copy(tiles_ref.at[part], held_ref.at[part], in_sem.at[i])

    for i in range(8):
        load(i).start()
    for i in range(8):
        load(i).wait()
        for j in range(i * chunk, (i + 1) * chunk):
            row = pl.multiple_of(rank_ref[j] * BLK, BLK)
            pltpu.make_async_copy(held_ref.at[j], out_ref.at[owner_ref[j], pl.ds(row, BLK)], out_sem).start()
    pltpu.make_async_copy(tiles_ref, held_ref, out_sem).wait()
    notes.wait()


def spread(owner, rank, tiles, notes):
    devices = notes.shape[0]
    smem = pl.BlockSpec(memory_space=pltpu.SMEM)
    return pl.pallas_call(
        spread_kernel,
        out_shape=jax.ShapeDtypeStruct((devices, 2 * BLK + 8, BLK), jnp.float32),
        in_specs=[smem, smem, ANY, ANY],
        out_specs=ANY,
        scratch_shapes=[
            pltpu.VMEM((TILES_DEV, BLK, BLK), jnp.float32),
            pltpu.SemaphoreType.DMA((8,)),
            pltpu.SemaphoreType.DMA,
            pltpu.SemaphoreType.DMA,
        ],
        compiler_params=pltpu.CompilerParams(vmem_limit_bytes=60 << 20),
        name="spread",
    )(owner, rank, tiles, notes)


def sum_kernel(slot_ref, arrived_ref, out_ref):
    step = pl.program_id(0)

    @pl.when(step == 0)
    def _():
        out_ref[...] = jnp.zeros_like(out_ref)

    for t in range(SUM_GROUP):
        for rank in range(2):
            slot = slot_ref[2 * (step * SUM_GROUP + t) + rank]

            @pl.when(slot >= 0)
            def _(t=t, rank=rank, slot=slot):
                out_ref[slot] = out_ref[slot] + arrived_ref[t, rank * BLK : (rank + 1) * BLK]


def slot_sums(slot, arrived):
    count, rows, _ = arrived.shape
    return pl.pallas_call(
        sum_kernel,
        out_shape=jax.ShapeDtypeStruct((SLOTS, BLK, BLK), jnp.float32),
        grid_spec=pltpu.PrefetchScalarGridSpec(
            num_scalar_prefetch=1,
            grid=(count // SUM_GROUP,),
            in_specs=[pl.BlockSpec((SUM_GROUP, rows, BLK), lambda i, slot_ref: (i, 0, 0))],
            out_specs=pl.BlockSpec((SLOTS, BLK, BLK), lambda i, slot_ref: (0, 0, 0)),
        ),
        compiler_params=pltpu.CompilerParams(vmem_limit_bytes=16 << 20),
        name="slot_sums",
    )(slot, arrived)


def body(pivot_block, border, trailing, dest_owner, dest_slot, row_map):
    member = lax.axis_index("grid")
    devices = lax.axis_size("front") * lax.axis_size("grid")
    listed = dest_owner.shape[1]
    pivot_factor, border_factor, tiles = front_tiles(pivot_block[0], border[0], trailing[0], row_map[0])
    owner = dest_owner[0, :, 0]
    place = jnp.arange(listed, dtype=jnp.int32)
    same = (owner[:, None] == owner[None, :]) & (place[None, :] < place[:, None])
    rank = jnp.any(same, axis=1).astype(jnp.int32)
    slot = jnp.where(place < 100 + 4 * member, dest_slot[0] + 1, 0)
    hits = owner[None, :] == jnp.arange(devices, dtype=jnp.int32)[:, None]
    slots = [
        jnp.sum(jnp.where(hits & (rank == which)[None, :], slot[None, :], 0), axis=1).astype(jnp.float32)
        for which in range(2)
    ]
    lane = lax.broadcasted_iota(jnp.int32, (devices, 8, BLK), 2)
    notes = jnp.where(lane == 0, slots[0][:, None, None], jnp.where(lane == 1, slots[1][:, None, None], 0.0))
    outgoing = spread(owner, rank, tiles, notes)
    arrived = lax.all_to_all(outgoing, ("front", "grid"), split_axis=0, concat_axis=0, tiled=True)
    pivot_factor, border_factor, arrived = lax.optimization_barrier((pivot_factor, border_factor, arrived))
    slot_in = arrived[:, 2 * BLK, :2].astype(jnp.int32).reshape(-1) - 1
    sums = slot_sums(slot_in, arrived)
    return pivot_factor[None], border_factor[None], sums


def solution(mesh):
    return jax.shard_map(
        body,
        mesh=mesh,
        in_specs=(
            P("front", None, None),
            P("front", "grid", None),
            P("front", "grid", None),
            P("front", "grid", None),
            P("front", "grid"),
            P("front", "grid", None),
        ),
        out_specs=(
            P("front", None, None),
            P("front", "grid", None),
            P(("front", "grid"), None, None),
        ),
        check_vma=False,
    )
```

```python
import functools

import jax
import jax.numpy as jnp
import numpy as np
from jax import lax
from jax.experimental import pallas as pl
from jax.experimental.pallas import tpu as pltpu
from jax.sharding import PartitionSpec as P

BLK = 128
SLOTS = 64
N_GRID = 16
SIDE = 4
TILES_DEV = 160
SUM_GROUP = 8
SPREAD_GROUP = 8
P_SIZE = 512
HI = lax.Precision.HIGHEST
VMEM = pl.BlockSpec(memory_space=pltpu.VMEM)
ANY = pl.BlockSpec(memory_space=pl.ANY)
MESH = pl.DeviceIdType.MESH
HALF = P_SIZE // 2


def tdot(a, b):
    return lax.dot_general(a, b, (((0,), (0,)), ((), ())), precision=HI, preferred_element_type=jnp.float32)


def factor_diagonal(block):
    aug = jnp.concatenate([block, jnp.eye(BLK, dtype=jnp.float32)], axis=1)
    sub = lax.broadcasted_iota(jnp.int32, (8, BLK), 0)
    sub2 = lax.broadcasted_iota(jnp.int32, (8, 2 * BLK), 0)
    done = []
    for panel in range(BLK // 8):
        rows = aug[:8]
        cols = [jnp.broadcast_to(rows[:, 8 * panel + m : 8 * panel + m + 1], (8, BLK)) for m in range(8)]
        for i in range(8):
            inv = lax.rsqrt(jnp.broadcast_to(cols[i][i : i + 1], (8, BLK)))
            mult = jnp.where(sub > i, cols[i] * inv, 0.0)
            inv2 = jnp.concatenate([inv, inv], axis=1)
            mult2 = jnp.concatenate([mult, mult], axis=1)
            top = jnp.broadcast_to(rows[i : i + 1], (8, 2 * BLK)) * inv2
            rows = jnp.where(sub2 == i, top, rows - mult2 * top)
            for m in range(i + 1, 8):
                cols[m] = cols[m] - mult * (jnp.broadcast_to(cols[m][i : i + 1], (8, BLK)) * inv)
        done.append(rows)
        if panel < BLK // 8 - 1:
            left = rows[:, :BLK]
            update = tdot(left, rows)
            aug = aug[8:] - update[8 * (panel + 1) :]
    full = jnp.concatenate(done, axis=0)
    r = lax.broadcasted_iota(jnp.int32, (BLK, BLK), 0)
    c = lax.broadcasted_iota(jnp.int32, (BLK, BLK), 1)
    return jnp.where(r <= c, full[:, :BLK], 0.0), full[:, BLK:]


def front_kernel(
    a_ref, b_ref, t_ref, map_ref,
    pivot_ref, border_ref, out_ref,
    aug_ref, all_ref, left_ref, right_ref, tile_ref, moved_ref,
    send_sem, recv_sem, local_sem, tile_sem, moved_sem,
):
    front, member = lax.axis_index("front"), lax.axis_index("grid")
    place = (member % SIDE, member // SIDE)

    def at(offset):
        return (place[1] + offset[1]) % SIDE * SIDE + (place[0] + offset[0]) % SIDE

    def along(half, first, second):
        return (first, second) if half == 0 else (second, first)

    def piece(half, source, quarter):
        start, size = (half * HALF, HALF) if quarter is None else (half * HALF + quarter * BLK, BLK)
        return all_ref.at[source, pl.ds(start, size)]

    def copy(half, kind, source, quarter, target):
        part = piece(half, source, quarter)
        return pltpu.make_async_remote_copy(
            src_ref=part, dst_ref=part, send_sem=send_sem.at[half, kind], recv_sem=recv_sem.at[half, kind],
            device_id=(front, target), device_id_type=MESH,
        )

    def send(half, kind, first, second, quarter, step):
        copy(half, kind, at(along(half, first, second)), quarter, at(step)).start()

    def arrived(half, kind, first, second, quarter):
        copy(half, kind, at(along(half, first, second)), quarter, member).wait_recv()

    def open_own():
        for half in range(2):
            send(half, 0, 0, 0, None, along(half, 1, 0))
            send(half, 1, 0, 0, None, along(half, 3, 0))
        for half in range(2):
            second_axis(half, 0)

    def second_axis(half, d):
        send(half, 4 + d, d, 0, None, along(half, 0, 1))
        send(half, 8 + d, d, 0, None, along(half, 0, 3))

    def pass_on(half, d):
        arrived(half, 4 + d, d, 3, None)
        send(half, 12 + d, d, 3, 0, along(half, 0, 1))
        arrived(half, 8 + d, d, 1, None)
        send(half, 16 + d, d, 1, 1, along(half, 0, 3))

    def stage_first():
        for half in range(2):
            arrived(half, 0, 3, 0, None)
            send(half, 2, 3, 0, 0, along(half, 1, 0))
            arrived(half, 1, 1, 0, None)
            send(half, 3, 1, 0, 1, along(half, 3, 0))
        for half in range(2):
            second_axis(half, 3)
            second_axis(half, 1)

    def stage_second():
        for half in range(2):
            arrived(half, 2, 2, 0, 0)
            arrived(half, 3, 2, 0, 1)
            second_axis(half, 2)
        for half in range(2):
            pass_on(half, 0)

    def stage_third():
        for half in range(2):
            pass_on(half, 3)
            pass_on(half, 1)

    def stage_fourth():
        for half in range(2):
            pass_on(half, 2)

    barrier = pltpu.get_barrier_semaphore()
    neighbours = [at((1, 0)), at((3, 0)), at((0, 1)), at((0, 3))]
    for target in neighbours:
        pl.semaphore_signal(barrier, inc=1, device_id=(front, target), device_id_type=MESH)
    own = pltpu.make_async_copy(b_ref, all_ref.at[member], local_sem)
    own.start()
    own.wait()
    pl.semaphore_wait(barrier, 4)
    open_own()

    r = lax.broadcasted_iota(jnp.int32, (P_SIZE, P_SIZE), 0)
    c = lax.broadcasted_iota(jnp.int32, (P_SIZE, P_SIZE), 1)
    aug_ref[:, :P_SIZE] = a_ref[...]
    aug_ref[:, P_SIZE:] = jnp.where(r == c, 1.0, 0.0)
    lane = lax.broadcasted_iota(jnp.int32, (BLK, 2 * P_SIZE), 1)

    def step(b, _):
        start = pl.multiple_of(b * BLK, BLK)
        stripe = aug_ref[pl.ds(start, BLK), :]
        diag = aug_ref[pl.ds(start, BLK), pl.ds(start, BLK)]
        upper, inverse = factor_diagonal(diag)
        solved = jnp.dot(inverse, stripe, precision=HI, preferred_element_type=jnp.float32)
        solved = jnp.where(lane >= start, solved, 0.0)
        aug_ref[pl.ds(start, BLK), :] = solved
        aug_ref[pl.ds(start, BLK), pl.ds(start, BLK)] = upper

        def rest(k, _):
            row = pl.multiple_of(k * BLK, BLK)
            left = aug_ref[pl.ds(start, BLK), pl.ds(row, BLK)]
            aug_ref[pl.ds(row, BLK), :] = aug_ref[pl.ds(row, BLK), :] - tdot(left, aug_ref[pl.ds(start, BLK), :])
            return 0

        lax.fori_loop(b + 1, P_SIZE // BLK, rest, 0)
        for when, stage in enumerate((stage_first, stage_second, stage_third, stage_fourth)):
            pl.when(b == when)(stage)
        return 0

    lax.fori_loop(0, P_SIZE // BLK, step, 0)

    def source_of(i):
        u, v = i % SIDE, i // SIDE
        rx = u + u // 2 - 2 * (u // 3)
        ry = v + v // 2 - 2 * (v // 3)
        return at((rx, ry)), rx, ry, u, v

    def tile_copy(i, slot):
        column = pl.multiple_of(source_of(i)[0] * P_SIZE, P_SIZE)
        return pltpu.make_async_copy(t_ref.at[:, pl.ds(column, P_SIZE)], tile_ref.at[slot], tile_sem.at[slot])

    tile_copy(0, 0).start()
    inverse = jnp.where(r >= c, aug_ref[:, P_SIZE:], 0.0)
    pivot_ref[...] = jnp.where(r >= c, aug_ref[:, :P_SIZE].T, 0.0)
    own_rows = all_ref[member]
    solved = lax.dot_general(own_rows, inverse, (((1,), (1,)), ((), ())), precision=HI, preferred_element_type=jnp.float32)
    border_ref[...] = solved
    weights = jnp.dot(solved, inverse, precision=HI, preferred_element_type=jnp.float32)
    high = weights.astype(jnp.bfloat16)
    left_ref[:, :P_SIZE] = high
    left_ref[:, P_SIZE : 2 * P_SIZE] = high
    left_ref[:, 2 * P_SIZE :] = (weights - high.astype(jnp.float32)).astype(jnp.bfloat16)

    def moved_wait(slot):
        pltpu.make_async_copy(moved_ref.at[slot], out_ref.at[pl.ds(0, 10)], moved_sem.at[slot]).wait()

    def source_step(i, _):
        slot = i % 2
        source, rx, ry, u, v = source_of(i)

        @pl.when(i + 1 < N_GRID)
        def _():
            tile_copy(i + 1, 1 - slot).start()

        @pl.when(u == 3)
        def _():
            arrived(1, 12 + ry, ry, 2, 0)
            arrived(1, 16 + ry, ry, 2, 1)

        @pl.when(v == 3)
        def _():
            arrived(0, 12 + rx, rx, 2, 0)
            arrived(0, 16 + rx, rx, 2, 1)

        rows = all_ref[source]
        upper = rows.astype(jnp.bfloat16)
        right_ref[:, :P_SIZE] = upper
        right_ref[:, P_SIZE : 2 * P_SIZE] = (rows - upper.astype(jnp.float32)).astype(jnp.bfloat16)
        right_ref[:, 2 * P_SIZE :] = upper
        tile_copy(i, slot).wait()

        @pl.when(i >= 2)
        def _():
            moved_wait(slot)

        past = (source - member + N_GRID - 1) // N_GRID
        full = source - past * (source - member - 1)
        listed = 100 + 4 * member
        count = 0
        for pair in range(2):
            low = pair * HALF
            product = lax.dot_general(
                left_ref[low:, :], right_ref[low : low + HALF, :], (((1,), (1,)), ((), ())),
                preferred_element_type=jnp.float32,
            )
            tile_ref[slot, low:, low : low + HALF] = tile_ref[slot, low:, low : low + HALF] - product
            for k in range(2 * pair, 4):
                for m in range(2 * pair, min(2 * pair + 1, k) + 1):
                    entry = 8 * k * (k - 1) + k * (member + 1) + source * k + full + m
                    if m == k:
                        entry = entry + past * (listed + k * (N_GRID - 1 - member) + source - member - 1 - entry)
                    value = tile_ref[slot, k * BLK : (k + 1) * BLK, m * BLK : (m + 1) * BLK]
                    first = value.astype(jnp.bfloat16)
                    last = (value - first.astype(jnp.float32)).astype(jnp.bfloat16)
                    wanted = jnp.broadcast_to(map_ref[pl.ds(entry, 1), :], (BLK, BLK))
                    chosen = wanted == lax.broadcasted_iota(jnp.int32, (BLK, BLK), 0)
                    chosen = jnp.where(chosen, 1.0, 0.0).astype(jnp.bfloat16)
                    moved = lax.dot_general(
                        chosen, jnp.concatenate([first, last], axis=1), (((0,), (0,)), ((), ())),
                        preferred_element_type=jnp.float32,
                    )
                    moved_ref[slot, count] = moved[:, :BLK] + moved[:, BLK:]
                    pltpu.make_async_copy(moved_ref.at[slot, count], out_ref.at[entry], moved_sem.at[slot]).start()
                    count += 1
        return 0

    lax.fori_loop(0, N_GRID, source_step, 0)
    moved_wait(0)
    moved_wait(1)
    for half in range(2):
        for kind in range(20):
            quarter = None if kind < 2 or 4 <= kind < 12 else 0
            copy(half, kind, member, quarter, member).wait_send()


def front_tiles(pivot_block, border, trailing, row_map):
    square = jax.ShapeDtypeStruct((P_SIZE, P_SIZE), jnp.float32)
    return pl.pallas_call(
        front_kernel,
        out_shape=(square, square, jax.ShapeDtypeStruct((TILES_DEV, BLK, BLK), jnp.float32)),
        in_specs=[VMEM, ANY, ANY, VMEM],
        out_specs=(VMEM, VMEM, ANY),
        scratch_shapes=[
            pltpu.VMEM((P_SIZE, 2 * P_SIZE), jnp.float32),
            pltpu.VMEM((N_GRID, P_SIZE, P_SIZE), jnp.float32),
            pltpu.VMEM((P_SIZE, 3 * P_SIZE), jnp.bfloat16),
            pltpu.VMEM((P_SIZE, 3 * P_SIZE), jnp.bfloat16),
            pltpu.VMEM((2, P_SIZE, P_SIZE), jnp.float32),
            pltpu.VMEM((2, 10, BLK, BLK), jnp.float32),
            pltpu.SemaphoreType.DMA((2, 20)),
            pltpu.SemaphoreType.DMA((2, 20)),
            pltpu.SemaphoreType.DMA,
            pltpu.SemaphoreType.DMA((2,)),
            pltpu.SemaphoreType.DMA((2,)),
        ],
        compiler_params=pltpu.CompilerParams(collective_id=0, has_side_effects=True, vmem_limit_bytes=52 << 20),
        name="front_tiles",
    )(pivot_block, border, trailing, row_map)


def spread_kernel(entry_ref, tiles_ref, note_ref, out_ref):
    step = pl.program_id(0)
    for t in range(SPREAD_GROUP):
        for rank in range(2):
            entry = entry_ref[2 * (step * SPREAD_GROUP + t) + rank]

            @pl.when(entry >= 0)
            def _(t=t, rank=rank, entry=entry):
                out_ref[t, rank * BLK : (rank + 1) * BLK] = tiles_ref[entry]

        out_ref[t, 2 * BLK :] = note_ref[t]


def spread(entry, tiles, notes):
    devices = notes.shape[0]
    return pl.pallas_call(
        spread_kernel,
        out_shape=jax.ShapeDtypeStruct((devices, 2 * BLK + 8, BLK), jnp.float32),
        grid_spec=pltpu.PrefetchScalarGridSpec(
            num_scalar_prefetch=1,
            grid=(devices // SPREAD_GROUP,),
            in_specs=[
                pl.BlockSpec((TILES_DEV, BLK, BLK), lambda i, entry_ref: (0, 0, 0), pipeline_mode=pl.Buffered(1)),
                pl.BlockSpec((SPREAD_GROUP, 8, BLK), lambda i, entry_ref: (i, 0, 0)),
            ],
            out_specs=pl.BlockSpec((SPREAD_GROUP, 2 * BLK + 8, BLK), lambda i, entry_ref: (i, 0, 0)),
        ),
        compiler_params=pltpu.CompilerParams(vmem_limit_bytes=60 << 20),
        name="spread",
    )(entry, tiles, notes)


def sum_kernel(whole_ref, arrived_ref, out_ref, note_ref, sem):
    step = pl.program_id(0)

    @pl.when(step == 0)
    def _():
        notes = pltpu.make_async_copy(whole_ref.at[:, pl.ds(2 * BLK, 1)], note_ref, sem)
        notes.start()
        out_ref[...] = jnp.zeros_like(out_ref)
        notes.wait()

    for t in range(SUM_GROUP):
        for rank in range(2):
            slot = note_ref[step * SUM_GROUP + t, 0, rank].astype(jnp.int32) - 1

            @pl.when(slot >= 0)
            def _(t=t, rank=rank, slot=slot):
                out_ref[slot] = out_ref[slot] + arrived_ref[t, rank * BLK : (rank + 1) * BLK]


def slot_sums(arrived):
    count, rows, _ = arrived.shape
    return pl.pallas_call(
        sum_kernel,
        out_shape=jax.ShapeDtypeStruct((SLOTS, BLK, BLK), jnp.float32),
        grid=(count // SUM_GROUP,),
        in_specs=[ANY, pl.BlockSpec((SUM_GROUP, rows, BLK), lambda i: (i, 0, 0))],
        out_specs=pl.BlockSpec((SLOTS, BLK, BLK), lambda i: (0, 0, 0)),
        scratch_shapes=[pltpu.SMEM((count, 1, BLK), jnp.float32), pltpu.SemaphoreType.DMA],
        compiler_params=pltpu.CompilerParams(vmem_limit_bytes=16 << 20),
        name="slot_sums",
    )(arrived, arrived)


def body(pivot_block, border, trailing, dest_owner, dest_slot, row_map):
    member = lax.axis_index("grid")
    devices = lax.axis_size("front") * lax.axis_size("grid")
    listed = dest_owner.shape[1]
    pivot_factor, border_factor, tiles = front_tiles(pivot_block[0], border[0], trailing[0], row_map[0])
    owner = dest_owner[0, :, 0]
    place = jnp.arange(listed, dtype=jnp.int32)
    same = (owner[:, None] == owner[None, :]) & (place[None, :] < place[:, None])
    rank = jnp.any(same, axis=1).astype(jnp.int32)
    slot = jnp.where(place < 100 + 4 * member, dest_slot[0] + 1, 0)
    hits = owner[None, :] == jnp.arange(devices, dtype=jnp.int32)[:, None]
    chosen = [hits & (rank == which)[None, :] for which in range(2)]
    slots = [jnp.sum(jnp.where(c, slot[None, :], 0), axis=1).astype(jnp.float32) for c in chosen]
    entry = [jnp.sum(jnp.where(c, place[None, :] + 1, 0), axis=1) - 1 for c in chosen]
    lane = lax.broadcasted_iota(jnp.int32, (devices, 8, BLK), 2)
    notes = jnp.where(lane == 0, slots[0][:, None, None], jnp.where(lane == 1, slots[1][:, None, None], 0.0))
    outgoing = spread(jnp.stack(entry, axis=1).reshape(-1), tiles, notes)
    arrived = lax.all_to_all(outgoing, ("front", "grid"), split_axis=0, concat_axis=0, tiled=True)
    pivot_factor, border_factor, arrived = lax.optimization_barrier((pivot_factor, border_factor, arrived))
    sums = slot_sums(arrived)
    return pivot_factor[None], border_factor[None], sums


def solution(mesh):
    return jax.shard_map(
        body,
        mesh=mesh,
        in_specs=(
            P("front", None, None),
            P("front", "grid", None),
            P("front", "grid", None),
            P("front", "grid", None),
            P("front", "grid"),
            P("front", "grid", None),
        ),
        out_specs=(
            P("front", None, None),
            P("front", "grid", None),
            P(("front", "grid"), None, None),
        ),
        check_vma=False,
    )
```

```python
import functools

import jax
import jax.numpy as jnp
import numpy as np
from jax import lax
from jax.experimental import pallas as pl
from jax.experimental.pallas import tpu as pltpu
from jax.sharding import PartitionSpec as P

BLK = 128
SLOTS = 64
N_GRID = 16
SIDE = 4
TILES_DEV = 160
SUM_GROUP = 8
SPREAD_GROUP = 8
P_SIZE = 512
HI = lax.Precision.HIGHEST
VMEM = pl.BlockSpec(memory_space=pltpu.VMEM)
ANY = pl.BlockSpec(memory_space=pl.ANY)
MESH = pl.DeviceIdType.MESH
HALF = P_SIZE // 2


def tdot(a, b):
    return lax.dot_general(a, b, (((0,), (0,)), ((), ())), precision=HI, preferred_element_type=jnp.float32)


def split3(a):
    first = a.astype(jnp.bfloat16).astype(jnp.float32)
    second = (a - first).astype(jnp.bfloat16).astype(jnp.float32)
    return first, second, a - first - second


def outer8(a, b):
    a1, a2, a3 = split3(a)
    b1, b2, b3 = split3(b)
    left = jnp.concatenate([a1, a1, a2, a2, a1, a3], axis=0).astype(jnp.bfloat16)
    right = jnp.concatenate([b1, b2, b1, b2, b3, b1], axis=0).astype(jnp.bfloat16)
    return lax.dot_general(left, right, (((0,), (0,)), ((), ())), preferred_element_type=jnp.float32)


def factor_diagonal(block):
    aug = jnp.concatenate([block, jnp.eye(BLK, dtype=jnp.float32)], axis=1)
    sub = lax.broadcasted_iota(jnp.int32, (8, BLK), 0)
    sub2 = lax.broadcasted_iota(jnp.int32, (8, 2 * BLK), 0)
    done = []
    for panel in range(BLK // 8):
        rows = aug[:8]
        cols = [jnp.broadcast_to(rows[:, 8 * panel + m : 8 * panel + m + 1], (8, BLK)) for m in range(8)]
        for i in range(8):
            inv = lax.rsqrt(jnp.broadcast_to(cols[i][i : i + 1], (8, BLK)))
            mult = jnp.where(sub > i, cols[i] * inv, 0.0)
            inv2 = jnp.concatenate([inv, inv], axis=1)
            mult2 = jnp.concatenate([mult, mult], axis=1)
            top = jnp.broadcast_to(rows[i : i + 1], (8, 2 * BLK)) * inv2
            rows = jnp.where(sub2 == i, top, rows - mult2 * top)
            for m in range(i + 1, 8):
                cols[m] = cols[m] - mult * (jnp.broadcast_to(cols[m][i : i + 1], (8, BLK)) * inv)
        done.append(rows)
        if panel < BLK // 8 - 1:
            left = rows[:, :BLK]
            update = outer8(left, rows)
            aug = aug[8:] - update[8 * (panel + 1) :]
    full = jnp.concatenate(done, axis=0)
    r = lax.broadcasted_iota(jnp.int32, (BLK, BLK), 0)
    c = lax.broadcasted_iota(jnp.int32, (BLK, BLK), 1)
    return jnp.where(r <= c, full[:, :BLK], 0.0), full[:, BLK:]


def front_kernel(
    a_ref, b_ref, t_ref, map_ref,
    pivot_ref, border_ref, out_ref,
    aug_ref, all_ref, left_ref, right_ref, tile_ref, moved_ref,
    send_sem, recv_sem, local_sem, tile_sem, moved_sem,
):
    front, member = lax.axis_index("front"), lax.axis_index("grid")
    place = (member % SIDE, member // SIDE)

    def at(offset):
        return (place[1] + offset[1]) % SIDE * SIDE + (place[0] + offset[0]) % SIDE

    def along(half, first, second):
        return (first, second) if half == 0 else (second, first)

    def piece(half, source, quarter):
        start, size = (half * HALF, HALF) if quarter is None else (half * HALF + quarter * BLK, BLK)
        return all_ref.at[source, pl.ds(start, size)]

    def copy(half, kind, source, quarter, target):
        part = piece(half, source, quarter)
        return pltpu.make_async_remote_copy(
            src_ref=part, dst_ref=part, send_sem=send_sem.at[half, kind], recv_sem=recv_sem.at[half, kind],
            device_id=(front, target), device_id_type=MESH,
        )

    def send(half, kind, first, second, quarter, step):
        copy(half, kind, at(along(half, first, second)), quarter, at(step)).start()

    def arrived(half, kind, first, second, quarter):
        copy(half, kind, at(along(half, first, second)), quarter, member).wait_recv()

    def open_own():
        for half in range(2):
            send(half, 0, 0, 0, None, along(half, 1, 0))
            send(half, 1, 0, 0, None, along(half, 3, 0))
        for half in range(2):
            second_axis(half, 0)

    def second_axis(half, d):
        send(half, 4 + d, d, 0, None, along(half, 0, 1))
        send(half, 8 + d, d, 0, None, along(half, 0, 3))

    def pass_on(half, d):
        arrived(half, 4 + d, d, 3, None)
        send(half, 12 + d, d, 3, 0, along(half, 0, 1))
        arrived(half, 8 + d, d, 1, None)
        send(half, 16 + d, d, 1, 1, along(half, 0, 3))

    def stage_first():
        for half in range(2):
            arrived(half, 0, 3, 0, None)
            send(half, 2, 3, 0, 0, along(half, 1, 0))
            arrived(half, 1, 1, 0, None)
            send(half, 3, 1, 0, 1, along(half, 3, 0))
        for half in range(2):
            second_axis(half, 3)
            second_axis(half, 1)

    def stage_second():
        for half in range(2):
            arrived(half, 2, 2, 0, 0)
            arrived(half, 3, 2, 0, 1)
            second_axis(half, 2)
        for half in range(2):
            pass_on(half, 0)

    def stage_third():
        for half in range(2):
            pass_on(half, 3)
            pass_on(half, 1)

    def stage_fourth():
        for half in range(2):
            pass_on(half, 2)

    barrier = pltpu.get_barrier_semaphore()
    neighbours = [at((1, 0)), at((3, 0)), at((0, 1)), at((0, 3))]
    for target in neighbours:
        pl.semaphore_signal(barrier, inc=1, device_id=(front, target), device_id_type=MESH)
    own = pltpu.make_async_copy(b_ref, all_ref.at[member], local_sem)
    own.start()
    own.wait()
    pl.semaphore_wait(barrier, 4)
    open_own()

    r = lax.broadcasted_iota(jnp.int32, (P_SIZE, P_SIZE), 0)
    c = lax.broadcasted_iota(jnp.int32, (P_SIZE, P_SIZE), 1)
    aug_ref[:, :P_SIZE] = a_ref[...]
    aug_ref[:, P_SIZE:] = jnp.where(r == c, 1.0, 0.0)
    lane = lax.broadcasted_iota(jnp.int32, (BLK, 2 * P_SIZE), 1)

    def step(b, _):
        start = pl.multiple_of(b * BLK, BLK)
        stripe = aug_ref[pl.ds(start, BLK), :]
        diag = aug_ref[pl.ds(start, BLK), pl.ds(start, BLK)]
        upper, inverse = factor_diagonal(diag)
        solved = jnp.dot(inverse, stripe, precision=HI, preferred_element_type=jnp.float32)
        solved = jnp.where(lane >= start, solved, 0.0)
        aug_ref[pl.ds(start, BLK), :] = solved
        aug_ref[pl.ds(start, BLK), pl.ds(start, BLK)] = upper

        def rest(k, _):
            row = pl.multiple_of(k * BLK, BLK)
            left = aug_ref[pl.ds(start, BLK), pl.ds(row, BLK)]
            aug_ref[pl.ds(row, BLK), :] = aug_ref[pl.ds(row, BLK), :] - tdot(left, aug_ref[pl.ds(start, BLK), :])
            return 0

        lax.fori_loop(b + 1, P_SIZE // BLK, rest, 0)
        pl.when(b == 1)(stage_first)
        pl.when(b == 3)(stage_second)
        return 0

    lax.fori_loop(0, P_SIZE // BLK, step, 0)

    def source_of(i):
        late = i // 9
        odd, k = (i - 9) * late % 2, (i - 9) * late // 2
        u = (1 - late) * (i % 3) + late * (3 - odd * (3 - k))
        v = (1 - late) * (i // 3) + late * (k + odd * (3 - k))
        rx = u + u // 2 - 2 * (u // 3)
        ry = v + v // 2 - 2 * (v // 3)
        return at((rx, ry)), rx, ry, u, v

    def tile_copy(i, slot):
        column = pl.multiple_of(source_of(i)[0] * P_SIZE, P_SIZE)
        return pltpu.make_async_copy(t_ref.at[:, pl.ds(column, P_SIZE)], tile_ref.at[slot], tile_sem.at[slot])

    tile_copy(0, 0).start()
    inverse = jnp.where(r >= c, aug_ref[:, P_SIZE:], 0.0)
    pivot_ref[...] = jnp.where(r >= c, aug_ref[:, :P_SIZE].T, 0.0)
    own_rows = all_ref[member]
    solved = lax.dot_general(own_rows, inverse, (((1,), (1,)), ((), ())), precision=HI, preferred_element_type=jnp.float32)
    border_ref[...] = solved
    weights = jnp.dot(solved, inverse, precision=HI, preferred_element_type=jnp.float32)
    high = weights.astype(jnp.bfloat16)
    left_ref[:, :P_SIZE] = high
    left_ref[:, P_SIZE : 2 * P_SIZE] = high
    left_ref[:, 2 * P_SIZE :] = (weights - high.astype(jnp.float32)).astype(jnp.bfloat16)

    def moved_wait(slot):
        pltpu.make_async_copy(moved_ref.at[slot], out_ref.at[pl.ds(0, 10)], moved_sem.at[slot]).wait()

    def source_step(i, _):
        slot = i % 2
        source, rx, ry, u, v = source_of(i)

        @pl.when(i + 1 < N_GRID)
        def _():
            tile_copy(i + 1, 1 - slot).start()

        pl.when(i == 2)(stage_third)
        pl.when(i == 5)(stage_fourth)

        @pl.when(u == 3)
        def _():
            arrived(1, 12 + ry, ry, 2, 0)
            arrived(1, 16 + ry, ry, 2, 1)

        @pl.when(v == 3)
        def _():
            arrived(0, 12 + rx, rx, 2, 0)
            arrived(0, 16 + rx, rx, 2, 1)

        rows = all_ref[source]
        upper = rows.astype(jnp.bfloat16)
        right_ref[:, :P_SIZE] = upper
        right_ref[:, P_SIZE : 2 * P_SIZE] = (rows - upper.astype(jnp.float32)).astype(jnp.bfloat16)
        right_ref[:, 2 * P_SIZE :] = upper
        tile_copy(i, slot).wait()

        @pl.when(i >= 2)
        def _():
            moved_wait(slot)

        past = (source - member + N_GRID - 1) // N_GRID
        full = source - past * (source - member - 1)
        listed = 100 + 4 * member
        count = 0
        for pair in range(2):
            low = pair * HALF
            product = lax.dot_general(
                left_ref[low:, :], right_ref[low : low + HALF, :], (((1,), (1,)), ((), ())),
                preferred_element_type=jnp.float32,
            )
            tile_ref[slot, low:, low : low + HALF] = tile_ref[slot, low:, low : low + HALF] - product
            for k in range(2 * pair, 4):
                for m in range(2 * pair, min(2 * pair + 1, k) + 1):
                    entry = 8 * k * (k - 1) + k * (member + 1) + source * k + full + m
                    if m == k:
                        entry = entry + past * (listed + k * (N_GRID - 1 - member) + source - member - 1 - entry)
                    value = tile_ref[slot, k * BLK : (k + 1) * BLK, m * BLK : (m + 1) * BLK]
                    first = value.astype(jnp.bfloat16)
                    last = (value - first.astype(jnp.float32)).astype(jnp.bfloat16)
                    wanted = jnp.broadcast_to(map_ref[pl.ds(entry, 1), :], (BLK, BLK))
                    chosen = wanted == lax.broadcasted_iota(jnp.int32, (BLK, BLK), 0)
                    chosen = jnp.where(chosen, 1.0, 0.0).astype(jnp.bfloat16)
                    moved = lax.dot_general(
                        chosen, jnp.concatenate([first, last], axis=1), (((0,), (0,)), ((), ())),
                        preferred_element_type=jnp.float32,
                    )
                    moved_ref[slot, count] = moved[:, :BLK] + moved[:, BLK:]
                    pltpu.make_async_copy(moved_ref.at[slot, count], out_ref.at[entry], moved_sem.at[slot]).start()
                    count += 1
        return 0

    lax.fori_loop(0, N_GRID, source_step, 0)
    moved_wait(0)
    moved_wait(1)
    for half in range(2):
        for kind in range(20):
            quarter = None if kind < 2 or 4 <= kind < 12 else 0
            copy(half, kind, member, quarter, member).wait_send()


def front_tiles(pivot_block, border, trailing, row_map):
    square = jax.ShapeDtypeStruct((P_SIZE, P_SIZE), jnp.float32)
    return pl.pallas_call(
        front_kernel,
        out_shape=(square, square, jax.ShapeDtypeStruct((TILES_DEV, BLK, BLK), jnp.float32)),
        in_specs=[VMEM, ANY, ANY, VMEM],
        out_specs=(VMEM, VMEM, ANY),
        scratch_shapes=[
            pltpu.VMEM((P_SIZE, 2 * P_SIZE), jnp.float32),
            pltpu.VMEM((N_GRID, P_SIZE, P_SIZE), jnp.float32),
            pltpu.VMEM((P_SIZE, 3 * P_SIZE), jnp.bfloat16),
            pltpu.VMEM((P_SIZE, 3 * P_SIZE), jnp.bfloat16),
            pltpu.VMEM((2, P_SIZE, P_SIZE), jnp.float32),
            pltpu.VMEM((2, 10, BLK, BLK), jnp.float32),
            pltpu.SemaphoreType.DMA((2, 20)),
            pltpu.SemaphoreType.DMA((2, 20)),
            pltpu.SemaphoreType.DMA,
            pltpu.SemaphoreType.DMA((2,)),
            pltpu.SemaphoreType.DMA((2,)),
        ],
        compiler_params=pltpu.CompilerParams(collective_id=0, has_side_effects=True, vmem_limit_bytes=52 << 20),
        name="front_tiles",
    )(pivot_block, border, trailing, row_map)


def spread_kernel(entry_ref, slot_ref, tiles_ref, out_ref):
    step = pl.program_id(0)
    lane = lax.broadcasted_iota(jnp.int32, (8, BLK), 1)
    for t in range(SPREAD_GROUP):
        at = 2 * (step * SPREAD_GROUP + t)
        for rank in range(2):
            entry = entry_ref[at + rank]

            @pl.when(entry >= 0)
            def _(t=t, rank=rank, entry=entry):
                out_ref[t, rank * BLK : (rank + 1) * BLK] = tiles_ref[entry]

        note = jnp.where(lane == 0, slot_ref[at], jnp.where(lane == 1, slot_ref[at + 1], 0))
        out_ref[t, 2 * BLK :] = note.astype(jnp.float32)


def spread(entry, slot, tiles):
    devices = entry.shape[0] // 2
    return pl.pallas_call(
        spread_kernel,
        out_shape=jax.ShapeDtypeStruct((devices, 2 * BLK + 8, BLK), jnp.float32),
        grid_spec=pltpu.PrefetchScalarGridSpec(
            num_scalar_prefetch=2,
            grid=(devices // SPREAD_GROUP,),
            in_specs=[pl.BlockSpec(memory_space=pltpu.VMEM)],
            out_specs=pl.BlockSpec((SPREAD_GROUP, 2 * BLK + 8, BLK), lambda i, entry_ref, slot_ref: (i, 0, 0)),
        ),
        compiler_params=pltpu.CompilerParams(vmem_limit_bytes=24 << 20),
        name="spread",
    )(entry, slot, tiles)


def sum_kernel(whole_ref, arrived_ref, out_ref, note_ref, sem):
    step = pl.program_id(0)

    @pl.when(step == 0)
    def _():
        notes = pltpu.make_async_copy(whole_ref.at[:, pl.ds(2 * BLK, 1)], note_ref, sem)
        notes.start()
        out_ref[...] = jnp.zeros_like(out_ref)
        notes.wait()

    for t in range(SUM_GROUP):
        for rank in range(2):
            slot = note_ref[step * SUM_GROUP + t, 0, rank].astype(jnp.int32) - 1

            @pl.when(slot >= 0)
            def _(t=t, rank=rank, slot=slot):
                out_ref[slot] = out_ref[slot] + arrived_ref[t, rank * BLK : (rank + 1) * BLK]


def slot_sums(arrived):
    count, rows, _ = arrived.shape
    return pl.pallas_call(
        sum_kernel,
        out_shape=jax.ShapeDtypeStruct((SLOTS, BLK, BLK), jnp.float32),
        grid=(count // SUM_GROUP,),
        in_specs=[ANY, pl.BlockSpec((SUM_GROUP, rows, BLK), lambda i: (i, 0, 0))],
        out_specs=pl.BlockSpec((SLOTS, BLK, BLK), lambda i: (0, 0, 0)),
        scratch_shapes=[pltpu.SMEM((count, 1, BLK), jnp.float32), pltpu.SemaphoreType.DMA],
        compiler_params=pltpu.CompilerParams(vmem_limit_bytes=16 << 20),
        name="slot_sums",
    )(arrived, arrived)


def body(pivot_block, border, trailing, dest_owner, dest_slot, row_map):
    member = lax.axis_index("grid")
    devices = lax.axis_size("front") * lax.axis_size("grid")
    listed = dest_owner.shape[1]
    pivot_factor, border_factor, tiles = front_tiles(pivot_block[0], border[0], trailing[0], row_map[0])
    owner = dest_owner[0, :, 0]
    place = jnp.arange(listed, dtype=jnp.int32)
    same = (owner[:, None] == owner[None, :]) & (place[None, :] < place[:, None])
    rank = jnp.any(same, axis=1).astype(jnp.int32)
    slot = jnp.where(place < 100 + 4 * member, dest_slot[0] + 1, 0)
    hits = owner[None, :] == jnp.arange(devices, dtype=jnp.int32)[:, None]
    chosen = [hits & (rank == which)[None, :] for which in range(2)]
    slots = [jnp.sum(jnp.where(c, slot[None, :], 0), axis=1) for c in chosen]
    entry = [jnp.sum(jnp.where(c, place[None, :] + 1, 0), axis=1) - 1 for c in chosen]
    outgoing = spread(jnp.stack(entry, axis=1).reshape(-1), jnp.stack(slots, axis=1).reshape(-1), tiles)
    arrived = lax.all_to_all(outgoing, ("front", "grid"), split_axis=0, concat_axis=0, tiled=True)
    pivot_factor, border_factor, arrived = lax.optimization_barrier((pivot_factor, border_factor, arrived))
    sums = slot_sums(arrived)
    return pivot_factor[None], border_factor[None], sums


def solution(mesh):
    return jax.shard_map(
        body,
        mesh=mesh,
        in_specs=(
            P("front", None, None),
            P("front", "grid", None),
            P("front", "grid", None),
            P("front", "grid", None),
            P("front", "grid"),
            P("front", "grid", None),
        ),
        out_specs=(
            P("front", None, None),
            P("front", "grid", None),
            P(("front", "grid"), None, None),
        ),
        check_vma=False,
    )
```

```python
import functools

import jax
import jax.numpy as jnp
import numpy as np
from jax import lax
from jax.experimental import pallas as pl
from jax.experimental.pallas import tpu as pltpu
from jax.sharding import PartitionSpec as P

BLK = 128
SLOTS = 64
N_GRID = 16
SIDE = 4
TILES_DEV = 160
SUM_GROUP = 16
SPREAD_GROUP = 16
P_SIZE = 512
HI = lax.Precision.HIGHEST
VMEM = pl.BlockSpec(memory_space=pltpu.VMEM)
ANY = pl.BlockSpec(memory_space=pl.ANY)
MESH = pl.DeviceIdType.MESH
HALF = P_SIZE // 2


def tdot(a, b):
    return lax.dot_general(a, b, (((0,), (0,)), ((), ())), precision=HI, preferred_element_type=jnp.float32)


def split3(a):
    first = a.astype(jnp.bfloat16).astype(jnp.float32)
    second = (a - first).astype(jnp.bfloat16).astype(jnp.float32)
    return first, second, a - first - second


def outer8(a, b):
    a1, a2, a3 = split3(a)
    b1, b2, b3 = split3(b)
    left = jnp.concatenate([a1, a1, a2, a2, a1, a3], axis=0).astype(jnp.bfloat16)
    right = jnp.concatenate([b1, b2, b1, b2, b3, b1], axis=0).astype(jnp.bfloat16)
    return lax.dot_general(left, right, (((0,), (0,)), ((), ())), preferred_element_type=jnp.float32)


def factor_diagonal(block):
    aug = jnp.concatenate([block, jnp.eye(BLK, dtype=jnp.float32)], axis=1)
    sub = lax.broadcasted_iota(jnp.int32, (8, BLK), 0)
    sub2 = lax.broadcasted_iota(jnp.int32, (8, 2 * BLK), 0)
    done = []
    for panel in range(BLK // 8):
        rows = aug[:8]
        cols = [jnp.broadcast_to(rows[:, 8 * panel + m : 8 * panel + m + 1], (8, BLK)) for m in range(8)]
        for i in range(8):
            inv = lax.rsqrt(jnp.broadcast_to(cols[i][i : i + 1], (8, BLK)))
            mult = jnp.where(sub > i, cols[i] * inv, 0.0)
            inv2 = jnp.concatenate([inv, inv], axis=1)
            mult2 = jnp.concatenate([mult, mult], axis=1)
            top = jnp.broadcast_to(rows[i : i + 1], (8, 2 * BLK)) * inv2
            rows = jnp.where(sub2 == i, top, rows - mult2 * top)
            for m in range(i + 1, 8):
                cols[m] = cols[m] - mult * (jnp.broadcast_to(cols[m][i : i + 1], (8, BLK)) * inv)
        done.append(rows)
        if panel < BLK // 8 - 1:
            left = rows[:, :BLK]
            update = outer8(left, rows)
            aug = aug[8:] - update[8 * (panel + 1) :]
    full = jnp.concatenate(done, axis=0)
    r = lax.broadcasted_iota(jnp.int32, (BLK, BLK), 0)
    c = lax.broadcasted_iota(jnp.int32, (BLK, BLK), 1)
    return jnp.where(r <= c, full[:, :BLK], 0.0), full[:, BLK:]


def front_kernel(
    a_ref, b_ref, t_ref, map_ref,
    pivot_ref, border_ref, out_ref,
    aug_ref, all_ref, left_ref, right_ref, tile_ref, moved_ref,
    send_sem, recv_sem, local_sem, tile_sem, moved_sem,
):
    front, member = lax.axis_index("front"), lax.axis_index("grid")
    place = (member % SIDE, member // SIDE)

    def at(offset):
        return (place[1] + offset[1]) % SIDE * SIDE + (place[0] + offset[0]) % SIDE

    def along(half, first, second):
        return (first, second) if half == 0 else (second, first)

    def piece(half, source, quarter):
        start, size = (half * HALF, HALF) if quarter is None else (half * HALF + quarter * BLK, BLK)
        return all_ref.at[source, pl.ds(start, size)]

    def copy(half, kind, source, quarter, target):
        part = piece(half, source, quarter)
        return pltpu.make_async_remote_copy(
            src_ref=part, dst_ref=part, send_sem=send_sem.at[half, kind], recv_sem=recv_sem.at[half, kind],
            device_id=(front, target), device_id_type=MESH,
        )

    def send(half, kind, first, second, quarter, step):
        copy(half, kind, at(along(half, first, second)), quarter, at(step)).start()

    def arrived(half, kind, first, second, quarter):
        copy(half, kind, at(along(half, first, second)), quarter, member).wait_recv()

    def open_own():
        for half in range(2):
            send(half, 0, 0, 0, None, along(half, 1, 0))
            send(half, 1, 0, 0, None, along(half, 3, 0))
        for half in range(2):
            second_axis(half, 0)

    def second_axis(half, d):
        send(half, 4 + d, d, 0, None, along(half, 0, 1))
        send(half, 8 + d, d, 0, None, along(half, 0, 3))

    def pass_on(half, d):
        arrived(half, 4 + d, d, 3, None)
        send(half, 12 + d, d, 3, 0, along(half, 0, 1))
        arrived(half, 8 + d, d, 1, None)
        send(half, 16 + d, d, 1, 1, along(half, 0, 3))

    def stage_first():
        for half in range(2):
            arrived(half, 0, 3, 0, None)
            send(half, 2, 3, 0, 0, along(half, 1, 0))
            arrived(half, 1, 1, 0, None)
            send(half, 3, 1, 0, 1, along(half, 3, 0))
        for half in range(2):
            second_axis(half, 3)
            second_axis(half, 1)

    def stage_second():
        for half in range(2):
            arrived(half, 2, 2, 0, 0)
            arrived(half, 3, 2, 0, 1)
            second_axis(half, 2)
        for half in range(2):
            pass_on(half, 0)

    def stage_third():
        for half in range(2):
            pass_on(half, 3)
            pass_on(half, 1)

    def stage_fourth():
        for half in range(2):
            pass_on(half, 2)

    barrier = pltpu.get_barrier_semaphore()
    neighbours = [at((1, 0)), at((3, 0)), at((0, 1)), at((0, 3))]
    for target in neighbours:
        pl.semaphore_signal(barrier, inc=1, device_id=(front, target), device_id_type=MESH)
    own = pltpu.make_async_copy(b_ref, all_ref.at[member], local_sem)
    own.start()
    own.wait()
    pl.semaphore_wait(barrier, 4)
    open_own()

    r = lax.broadcasted_iota(jnp.int32, (P_SIZE, P_SIZE), 0)
    c = lax.broadcasted_iota(jnp.int32, (P_SIZE, P_SIZE), 1)
    aug_ref[:, :P_SIZE] = a_ref[...]
    aug_ref[:, P_SIZE:] = jnp.where(r == c, 1.0, 0.0)
    lane = lax.broadcasted_iota(jnp.int32, (BLK, 2 * P_SIZE), 1)

    def step(b, _):
        start = pl.multiple_of(b * BLK, BLK)
        stripe = aug_ref[pl.ds(start, BLK), :]
        diag = aug_ref[pl.ds(start, BLK), pl.ds(start, BLK)]
        upper, inverse = factor_diagonal(diag)
        solved = jnp.dot(inverse, stripe, precision=HI, preferred_element_type=jnp.float32)
        solved = jnp.where(lane >= start, solved, 0.0)
        aug_ref[pl.ds(start, BLK), :] = solved
        aug_ref[pl.ds(start, BLK), pl.ds(start, BLK)] = upper

        def rest(k, _):
            row = pl.multiple_of(k * BLK, BLK)
            left = aug_ref[pl.ds(start, BLK), pl.ds(row, BLK)]
            aug_ref[pl.ds(row, BLK), :] = aug_ref[pl.ds(row, BLK), :] - tdot(left, aug_ref[pl.ds(start, BLK), :])
            return 0

        lax.fori_loop(b + 1, P_SIZE // BLK, rest, 0)
        pl.when(b == 1)(stage_first)
        pl.when(b == 3)(stage_second)
        return 0

    lax.fori_loop(0, P_SIZE // BLK, step, 0)

    def source_of(i):
        late = i // 9
        odd, k = (i - 9) * late % 2, (i - 9) * late // 2
        u = (1 - late) * (i % 3) + late * (3 - odd * (3 - k))
        v = (1 - late) * (i // 3) + late * (k + odd * (3 - k))
        rx = u + u // 2 - 2 * (u // 3)
        ry = v + v // 2 - 2 * (v // 3)
        return at((rx, ry)), rx, ry, u, v

    def tile_copy(i, slot):
        column = pl.multiple_of(source_of(i)[0] * P_SIZE, P_SIZE)
        return pltpu.make_async_copy(t_ref.at[:, pl.ds(column, P_SIZE)], tile_ref.at[slot], tile_sem.at[slot])

    tile_copy(0, 0).start()
    inverse = jnp.where(r >= c, aug_ref[:, P_SIZE:], 0.0)
    pivot_ref[...] = jnp.where(r >= c, aug_ref[:, :P_SIZE].T, 0.0)
    own_rows = all_ref[member]
    solved = lax.dot_general(own_rows, inverse, (((1,), (1,)), ((), ())), precision=HI, preferred_element_type=jnp.float32)
    border_ref[...] = solved
    weights = jnp.dot(solved, inverse, precision=HI, preferred_element_type=jnp.float32)
    high = weights.astype(jnp.bfloat16)
    left_ref[:, :P_SIZE] = high
    left_ref[:, P_SIZE : 2 * P_SIZE] = high
    left_ref[:, 2 * P_SIZE :] = (weights - high.astype(jnp.float32)).astype(jnp.bfloat16)

    def moved_wait(slot):
        pltpu.make_async_copy(moved_ref.at[slot], out_ref.at[pl.ds(0, 10)], moved_sem.at[slot]).wait()

    def source_step(i, _):
        slot = i % 2
        source, rx, ry, u, v = source_of(i)

        @pl.when(i + 1 < N_GRID)
        def _():
            tile_copy(i + 1, 1 - slot).start()

        pl.when(i == 2)(stage_third)
        pl.when(i == 5)(stage_fourth)

        @pl.when(u == 3)
        def _():
            arrived(1, 12 + ry, ry, 2, 0)
            arrived(1, 16 + ry, ry, 2, 1)

        @pl.when(v == 3)
        def _():
            arrived(0, 12 + rx, rx, 2, 0)
            arrived(0, 16 + rx, rx, 2, 1)

        rows = all_ref[source]
        upper = rows.astype(jnp.bfloat16)
        right_ref[:, :P_SIZE] = upper
        right_ref[:, P_SIZE : 2 * P_SIZE] = (rows - upper.astype(jnp.float32)).astype(jnp.bfloat16)
        right_ref[:, 2 * P_SIZE :] = upper
        tile_copy(i, slot).wait()

        @pl.when(i >= 2)
        def _():
            moved_wait(slot)

        past = (source - member + N_GRID - 1) // N_GRID
        full = source - past * (source - member - 1)
        listed = 100 + 4 * member
        count = 0
        for pair in range(2):
            low = pair * HALF
            product = lax.dot_general(
                left_ref[low:, :], right_ref[low : low + HALF, :], (((1,), (1,)), ((), ())),
                preferred_element_type=jnp.float32,
            )
            tile_ref[slot, low:, low : low + HALF] = tile_ref[slot, low:, low : low + HALF] - product
            for k in range(2 * pair, 4):
                for m in range(2 * pair, min(2 * pair + 1, k) + 1):
                    entry = 8 * k * (k - 1) + k * (member + 1) + source * k + full + m
                    if m == k:
                        entry = entry + past * (listed + k * (N_GRID - 1 - member) + source - member - 1 - entry)
                    value = tile_ref[slot, k * BLK : (k + 1) * BLK, m * BLK : (m + 1) * BLK]
                    first = value.astype(jnp.bfloat16)
                    last = (value - first.astype(jnp.float32)).astype(jnp.bfloat16)
                    wanted = jnp.broadcast_to(map_ref[pl.ds(entry, 1), :], (BLK, BLK))
                    chosen = wanted == lax.broadcasted_iota(jnp.int32, (BLK, BLK), 0)
                    chosen = jnp.where(chosen, 1.0, 0.0).astype(jnp.bfloat16)
                    moved = lax.dot_general(
                        chosen, jnp.concatenate([first, last], axis=1), (((0,), (0,)), ((), ())),
                        preferred_element_type=jnp.float32,
                    )
                    moved_ref[slot, count] = moved[:, :BLK] + moved[:, BLK:]
                    pltpu.make_async_copy(moved_ref.at[slot, count], out_ref.at[entry], moved_sem.at[slot]).start()
                    count += 1
        return 0

    lax.fori_loop(0, N_GRID, source_step, 0)
    moved_wait(0)
    moved_wait(1)
    for half in range(2):
        for kind in range(20):
            quarter = None if kind < 2 or 4 <= kind < 12 else 0
            copy(half, kind, member, quarter, member).wait_send()


def front_tiles(pivot_block, border, trailing, row_map):
    square = jax.ShapeDtypeStruct((P_SIZE, P_SIZE), jnp.float32)
    return pl.pallas_call(
        front_kernel,
        out_shape=(square, square, jax.ShapeDtypeStruct((TILES_DEV, BLK, BLK), jnp.float32)),
        in_specs=[VMEM, ANY, ANY, VMEM],
        out_specs=(VMEM, VMEM, ANY),
        scratch_shapes=[
            pltpu.VMEM((P_SIZE, 2 * P_SIZE), jnp.float32),
            pltpu.VMEM((N_GRID, P_SIZE, P_SIZE), jnp.float32),
            pltpu.VMEM((P_SIZE, 3 * P_SIZE), jnp.bfloat16),
            pltpu.VMEM((P_SIZE, 3 * P_SIZE), jnp.bfloat16),
            pltpu.VMEM((2, P_SIZE, P_SIZE), jnp.float32),
            pltpu.VMEM((2, 10, BLK, BLK), jnp.float32),
            pltpu.SemaphoreType.DMA((2, 20)),
            pltpu.SemaphoreType.DMA((2, 20)),
            pltpu.SemaphoreType.DMA,
            pltpu.SemaphoreType.DMA((2,)),
            pltpu.SemaphoreType.DMA((2,)),
        ],
        compiler_params=pltpu.CompilerParams(collective_id=0, has_side_effects=True, vmem_limit_bytes=52 << 20),
        name="front_tiles",
    )(pivot_block, border, trailing, row_map)


def spread_kernel(entry_ref, slot_ref, tiles_ref, out_ref):
    step = pl.program_id(0)
    lane = lax.broadcasted_iota(jnp.int32, (8, BLK), 1)
    for t in range(SPREAD_GROUP):
        at = 2 * (step * SPREAD_GROUP + t)
        for rank in range(2):
            entry = entry_ref[at + rank]

            @pl.when(entry >= 0)
            def _(t=t, rank=rank, entry=entry):
                out_ref[t, rank * BLK : (rank + 1) * BLK] = tiles_ref[entry]

        note = jnp.where(lane == 0, slot_ref[at], jnp.where(lane == 1, slot_ref[at + 1], 0))
        out_ref[t, 2 * BLK :] = note.astype(jnp.float32)


def spread(entry, slot, tiles):
    devices = entry.shape[0] // 2
    return pl.pallas_call(
        spread_kernel,
        out_shape=jax.ShapeDtypeStruct((devices, 2 * BLK + 8, BLK), jnp.float32),
        grid_spec=pltpu.PrefetchScalarGridSpec(
            num_scalar_prefetch=2,
            grid=(devices // SPREAD_GROUP,),
            in_specs=[pl.BlockSpec(memory_space=pltpu.VMEM)],
            out_specs=pl.BlockSpec((SPREAD_GROUP, 2 * BLK + 8, BLK), lambda i, entry_ref, slot_ref: (i, 0, 0)),
        ),
        compiler_params=pltpu.CompilerParams(vmem_limit_bytes=24 << 20),
        name="spread",
    )(entry, slot, tiles)


def sum_kernel(whole_ref, arrived_ref, out_ref, note_ref, sem):
    step = pl.program_id(0)

    @pl.when(step == 0)
    def _():
        notes = pltpu.make_async_copy(whole_ref.at[:, pl.ds(2 * BLK, 1)], note_ref, sem)
        notes.start()
        out_ref[...] = jnp.zeros_like(out_ref)
        notes.wait()

    for t in range(SUM_GROUP):
        for rank in range(2):
            slot = note_ref[step * SUM_GROUP + t, 0, rank].astype(jnp.int32) - 1

            @pl.when(slot >= 0)
            def _(t=t, rank=rank, slot=slot):
                out_ref[slot] = out_ref[slot] + arrived_ref[t, rank * BLK : (rank + 1) * BLK]


def slot_sums(arrived):
    count, rows, _ = arrived.shape
    return pl.pallas_call(
        sum_kernel,
        out_shape=jax.ShapeDtypeStruct((SLOTS, BLK, BLK), jnp.float32),
        grid=(count // SUM_GROUP,),
        in_specs=[ANY, pl.BlockSpec((SUM_GROUP, rows, BLK), lambda i: (i, 0, 0))],
        out_specs=pl.BlockSpec((SLOTS, BLK, BLK), lambda i: (0, 0, 0)),
        scratch_shapes=[pltpu.SMEM((count, 1, BLK), jnp.float32), pltpu.SemaphoreType.DMA],
        compiler_params=pltpu.CompilerParams(vmem_limit_bytes=16 << 20),
        name="slot_sums",
    )(arrived, arrived)


def body(pivot_block, border, trailing, dest_owner, dest_slot, row_map):
    member = lax.axis_index("grid")
    devices = lax.axis_size("front") * lax.axis_size("grid")
    listed = dest_owner.shape[1]
    pivot_factor, border_factor, tiles = front_tiles(pivot_block[0], border[0], trailing[0], row_map[0])
    owner = dest_owner[0, :, 0]
    place = jnp.arange(listed, dtype=jnp.int32)
    same = (owner[:, None] == owner[None, :]) & (place[None, :] < place[:, None])
    rank = jnp.any(same, axis=1).astype(jnp.int32)
    slot = jnp.where(place < 100 + 4 * member, dest_slot[0] + 1, 0)
    hits = owner[None, :] == jnp.arange(devices, dtype=jnp.int32)[:, None]
    chosen = [hits & (rank == which)[None, :] for which in range(2)]
    slots = [jnp.sum(jnp.where(c, slot[None, :], 0), axis=1) for c in chosen]
    entry = [jnp.sum(jnp.where(c, place[None, :] + 1, 0), axis=1) - 1 for c in chosen]
    outgoing = spread(jnp.stack(entry, axis=1).reshape(-1), jnp.stack(slots, axis=1).reshape(-1), tiles)
    arrived = lax.all_to_all(outgoing, ("front", "grid"), split_axis=0, concat_axis=0, tiled=True)
    pivot_factor, border_factor, arrived = lax.optimization_barrier((pivot_factor, border_factor, arrived))
    sums = slot_sums(arrived)
    return pivot_factor[None], border_factor[None], sums


def solution(mesh):
    return jax.shard_map(
        body,
        mesh=mesh,
        in_specs=(
            P("front", None, None),
            P("front", "grid", None),
            P("front", "grid", None),
            P("front", "grid", None),
            P("front", "grid"),
            P("front", "grid", None),
        ),
        out_specs=(
            P("front", None, None),
            P("front", "grid", None),
            P(("front", "grid"), None, None),
        ),
        check_vma=False,
    )
```
